32 devices in a mesh: scan: 4 (over z), tx: 4 (over y, x), ty: 2 (over core).
Axes of the slice: x: 2, y: 2, z: 4, core: 2. Of those that a mesh axis runs over, the one named last changes fastest.
Arguments:
- object_slices: float32 [2, 2, 1024, 512], P(None, None, 'tx', 'ty'), may hold values from -0.9 to 0.9
- probe_modes: float32 [2, 8, 256, 256], replicated, may hold values from -1.2 to 1.2
- corners: int32 [4, 2, 4, 2], P('tx', 'ty', 'scan'), may hold values from 0 to 127, as said below
- measured: float32 [4, 2, 4, 256, 256], P('tx', 'ty', 'scan'), may hold values from 0.2 to 2.5
Outputs:
- updated_object: float32 [2, 2, 1024, 512], P(None, None, 'tx', 'ty')
The draws below stay inside these ranges and needn't reach their ends.
Inputs may be any that keep to these rules, and one draw needn't show every extreme that they name: corners place every window inside its own tile and the 128 pixels below and to the right of it.
All inputs are finite; a program needn't handle non-finite values.
Results may differ from the reference program's by a relative error of at most 0.0001.
Values sent between devices are 32-bit elements; how exact they have to be, the bound alone decides.
A program may use at most 64 MiB of HBM per device.

```python
import jax
import jax.numpy as jnp
from jax import lax

P_SIZE = 256
MODES = 8
SLICES = 2
ITERS = 1
TILE = 256
SCANS = 4
NY = 1024
NX = 512
N_TX = 4
N_TY = 2


def draw_corners(key, part):
    corner_span = TILE - P_SIZE + P_SIZE // 2
    drawn = jax.random.randint(key, (N_TX, N_TY, SCANS, 2), 0, corner_span, dtype=jnp.int32)
    drawn = drawn.at[0, 0, 0, :].set(0)
    return drawn.at[N_TX - 1, N_TY - 1, SCANS - 1, :].set(corner_span - 1)


def steps_of(own_key, extent, cuts, smallest, high):
    gain = 1.0
    for dim, parts in cuts:
        heights = jax.random.uniform(jax.random.fold_in(jax.random.fold_in(own_key, 6), dim), (parts,), jnp.float32, smallest / len(cuts), high / len(cuts))
        gain = gain * jnp.repeat(jnp.exp(heights), extent[dim] // parts).reshape((-1,) + (1,) * (len(extent) - 1 - dim))
    return gain


def scatter_about(rng, dims, width, limit, cuts=(), kind=jnp.bfloat16):
    gain = steps_of(rng, dims, cuts, -0.22, 0.18) if cuts else 1.0
    array = jax.random.normal(rng, dims, jnp.float32) * width * gain
    return jnp.minimum(jnp.maximum(array, -limit), limit).astype(kind)


def setup_inputs(seed: int = 0) -> dict:
    streams_of = jax.random.split(jax.random.key(seed), 5)
    return {
        "object_slices": scatter_about(streams_of[0], (SLICES, 2, NY, NX), 0.15, 0.9, ((2, 4), (3, 2)), jnp.float32),
        "probe_modes": scatter_about(streams_of[1], (2, MODES, P_SIZE, P_SIZE), 0.2, 1.2, (), jnp.float32),
        "corners": draw_corners(jax.random.fold_in(streams_of[4], 71), 0),
        "measured": jnp.clip(0.2 + 2.3 * jax.random.uniform(streams_of[3], (N_TX, N_TY, SCANS, P_SIZE, P_SIZE), jnp.float32) ** steps_of(streams_of[3], (N_TX, N_TY, SCANS, P_SIZE, P_SIZE), ((0, 4), (1, 2), (2, 4)), -0.2, 0.2), 0.2, 2.5),
    }


fresnel_coef = 0.1
step_size = 4.0


def laplacian(field):
    padded = jnp.pad(field, ((0, 0), (1, 1), (1, 1)))
    return padded[:, :-2, 1:-1] + padded[:, 2:, 1:-1] + padded[:, 1:-1, :-2] + padded[:, 1:-1, 2:] - 4.0 * field


def propagate(field, sign_value):
    lap_once = laplacian(field)
    lap_twice = laplacian(lap_once)
    return field + (sign_value * fresnel_coef * 1j) * lap_once - (0.5 * fresnel_coef ** 2) * lap_twice


def position_terms(padded_obj, probe_complex, row_start, col_start, measured_one):
    zero_index = jnp.zeros((), jnp.int32)
    window = lax.dynamic_slice(padded_obj, (zero_index, row_start, col_start), (SLICES, P_SIZE, P_SIZE))
    transmit = 1.0 + window
    stored = []
    field_now = probe_complex
    exit_wave = field_now
    for layer_index in range(SLICES):
        stored.append(field_now)
        exit_wave = field_now * transmit[layer_index]
        if layer_index + 1 < SLICES:
            field_now = propagate(exit_wave, 1.0)
    far_field = jnp.fft.fft2(exit_wave, norm="ortho")
    misfit = jnp.sum(jnp.real(far_field) ** 2 + jnp.imag(far_field) ** 2, axis=0) - measured_one
    backward = jnp.fft.ifft2(2.0 * misfit * far_field, norm="ortho")
    gradients = [None] * SLICES
    for layer_index in reversed(range(SLICES)):
        field_now = stored[layer_index]
        grad_term = jnp.sum(jnp.conj(field_now) * backward, axis=0)
        lighting = jnp.sum(jnp.real(field_now) ** 2 + jnp.imag(field_now) ** 2, axis=0)
        gradients[layer_index] = jnp.stack([jnp.real(grad_term), jnp.imag(grad_term), lighting])
        if layer_index > 0:
            backward = propagate(jnp.conj(transmit[layer_index]) * backward, -1.0)
    return jnp.stack(gradients)


def reference(object_slices, probe_modes, corners, measured):
    rim_width = P_SIZE // 2
    probe_complex = lax.complex(probe_modes[0], probe_modes[1])
    row_base = (jnp.arange(N_TX, dtype=jnp.int32) * TILE)[:, None, None]
    col_base = (jnp.arange(N_TY, dtype=jnp.int32) * TILE)[None, :, None]
    row_starts = (row_base + corners[..., 0]).reshape(-1).astype(jnp.int32)
    col_starts = (col_base + corners[..., 1]).reshape(-1).astype(jnp.int32)
    measured_flat = measured.reshape(-1, P_SIZE, P_SIZE)
    current = object_slices
    for iteration in range(ITERS):
        padded_obj = jnp.pad(lax.complex(current[:, 0], current[:, 1]), ((0, 0), (0, rim_width), (0, rim_width)))

        def visit(accumulated, item):
            row_start, col_start, measured_one = item
            grad_terms = position_terms(padded_obj, probe_complex, row_start, col_start, measured_one)
            zero_index = jnp.zeros((), jnp.int32)
            starts = (zero_index, zero_index, row_start, col_start)
            updated = lax.dynamic_slice(accumulated, starts, grad_terms.shape) + grad_terms
            return lax.dynamic_update_slice(accumulated, updated, starts), None

        initial = jnp.zeros((SLICES, 3, NY + rim_width, NX + rim_width), jnp.float32)
        accumulated = lax.scan(visit, initial, (row_starts, col_starts, measured_flat))[0]
        summed = accumulated[:, :, :NY, :NX]
        current = current - step_size * summed[:, :2] / (summed[:, 2:3] + 1.0)
    return current
```

```python
import functools
import math

import jax
import jax.numpy as jnp
import numpy as np
from jax import lax
from jax.experimental import pallas as pl
from jax.experimental.pallas import tpu as pltpu
from jax.sharding import PartitionSpec as P

fresnel_coef = 0.1
step_size = 4.0
damping = 0.5 * fresnel_coef**2


def dft_tables(pixels):
    half = pixels // 2
    tables = []
    for parity in range(2):
        freq = 2 * np.arange(half) + parity
        angle = 2.0 * np.pi * ((freq[:, None] * np.arange(half)[None, :]) % pixels) / pixels
        c, s = np.cos(angle) / math.sqrt(pixels), np.sin(angle) / math.sqrt(pixels)
        tables.append(np.block([[c, s], [-s, c]]))
    tables += [t.T for t in tables]
    out = []
    for t in tables:
        t32 = t.astype(np.float32)
        high = t32.astype(jnp.bfloat16)
        low = (t - high.astype(np.float64)).astype(np.float32).astype(jnp.bfloat16)
        out += [high, low]
    return np.stack(out)


def split2(x):
    high = x.astype(jnp.bfloat16)
    return high, (x - high.astype(jnp.float32)).astype(jnp.bfloat16)


def right_dot(x, high, low):
    xh, xl = split2(x)
    lhs = jnp.concatenate([xh, xl, xh], axis=1)
    rhs = jnp.concatenate([high, high, low], axis=0)
    return jnp.dot(lhs, rhs, preferred_element_type=jnp.float32)


def left_dot(high, low, x):
    xh, xl = split2(x)
    lhs = jnp.concatenate([high, high, low], axis=1)
    rhs = jnp.concatenate([xh, xl, xh], axis=0)
    return jnp.dot(lhs, rhs, preferred_element_type=jnp.float32)


def propagate(re, im, sign, edges):
    first_row, last_row, first_col, last_col = edges
    n = re.shape[0]

    def lap(v):
        up = jnp.where(first_row, 0.0, pltpu.roll(v, 1, 0))
        down = jnp.where(last_row, 0.0, pltpu.roll(v, n - 1, 0))
        left = jnp.where(first_col, 0.0, pltpu.roll(v, 1, 1))
        right = jnp.where(last_col, 0.0, pltpu.roll(v, n - 1, 1))
        return (up + down) + (left + right) - 4.0 * v

    l_re, l_im = lap(re), lap(im)
    ll_re, ll_im = lap(l_re), lap(l_im)
    coef = sign * fresnel_coef
    return re - coef * l_im - damping * ll_re, im + coef * l_re - damping * ll_im


MESH = pl.DeviceIdType.MESH
PIECES = 2


def iteration_kernel(
    n, n_tx, n_ty, corner, tile, probe_in, measured_in, tables_in, out,
    probe, measured, tables, ext0, ext1, trans, wave1, far, misfit, sums,
    work, ty_out, ty_in, tx_in, rs_in,
    local_sem, rim_send, rim_recv, r1_send, r1_recv, r2_send, r2_recv,
    rs_send, rs_recv, ag_send, ag_recv,
):
    me, tx, ty = lax.axis_index("scan"), lax.axis_index("tx"), lax.axis_index("ty")
    modes, pix = probe.shape[1], probe.shape[2]
    h = pix // 2
    side, wide = tile.shape[1], ext0.shape[1]
    rim = wide - side
    up, left = tx > 0, ty > 0
    down, right = tx + 1 < n_tx, ty + 1 < n_ty
    tx_up, ty_left = jnp.maximum(tx - 1, 0), jnp.maximum(ty - 1, 0)
    tx_down, ty_right = jnp.minimum(tx + 1, n_tx - 1), jnp.minimum(ty + 1, n_ty - 1)
    on_low = 2 * me < n
    step = jnp.where(on_low, 1, -1)
    outer = jnp.where(on_low, me > 0, me < n - 1)
    inward = jnp.clip(me + step, 0, n - 1)
    outward = jnp.clip(me - step, 0, n - 1)
    near_way = jnp.where(on_low, 0, 1)
    far_way = 1 - near_way

    barrier = pltpu.get_barrier_semaphore()
    neighbours = [
        (up, {"tx": tx_up}), (down, {"tx": tx_down}),
        (left, {"ty": ty_left}), (right, {"ty": ty_right}),
        (outer, {"scan": outward}), (me >= 0, {"scan": inward}),
    ]
    for there, target in neighbours:

        @pl.when(there)
        def _():
            pl.semaphore_signal(barrier, inc=1, device_id=target, device_id_type=MESH)

    exts = (ext0, ext1)
    loads = [
        pltpu.make_async_copy(probe_in, probe, local_sem.at[0]),
        pltpu.make_async_copy(measured_in, measured, local_sem.at[1]),
        pltpu.make_async_copy(tables_in, tables, local_sem.at[2]),
        pltpu.make_async_copy(
            tile.at[pl.ds(0, 2)], ext0.at[:, pl.ds(0, side), pl.ds(0, side)], local_sem.at[3]),
        pltpu.make_async_copy(
            tile.at[pl.ds(2, 2)], ext1.at[:, pl.ds(0, side), pl.ds(0, side)], local_sem.at[4]),
    ]
    for load in loads:
        load.start()

    r, c = corner[0], corner[1]
    up_roll = jnp.where(r == 0, 0, wide - r)
    left_roll = jnp.where(c == 0, 0, wide - c)

    def remote(source, place, sends, recvs, target):
        return pltpu.make_async_remote_copy(
            src_ref=source, dst_ref=place, send_sem=sends, recv_sem=recvs,
            device_id=target, device_id_type=MESH,
        )

    near, beyond, first = pl.ds(0, side), pl.ds(side, rim), pl.ds(0, rim)
    sideways, upward, corners = [], [], []
    for s in range(2):
        part, ext = tile.at[pl.ds(2 * s, 2)], exts[s]
        sideways.append(remote(
            part.at[:, :, first], ext.at[:, near, beyond],
            rim_send.at[s, 0], rim_recv.at[s, 0], {"ty": ty_left}))
        upward.append(remote(
            part.at[:, first, :], ext.at[:, beyond, near],
            rim_send.at[s, 1], rim_recv.at[s, 1], {"tx": tx_up}))
        corners.append(remote(
            ext.at[:, beyond, first], ext.at[:, beyond, beyond],
            rim_send.at[s, 2], rim_recv.at[s, 2], {"ty": ty_left}))

    for s in range(2):
        ext = exts[s]

        @pl.when(jnp.logical_not(right))
        def _():
            ext[:, near, beyond] = jnp.zeros((2, side, rim), jnp.float32)

        @pl.when(jnp.logical_not(down))
        def _():
            ext[:, beyond, near] = jnp.zeros((2, rim, side), jnp.float32)

        @pl.when(jnp.logical_not(right & down))
        def _():
            ext[:, beyond, beyond] = jnp.zeros((2, rim, rim), jnp.float32)

    sums[...] = jnp.zeros_like(sums)
    body = pl.ds(0, pix)

    row = lax.broadcasted_iota(jnp.int32, (pix, pix), 0)
    col = lax.broadcasted_iota(jnp.int32, (pix, pix), 1)
    edges = (row == 0, row == pix - 1, col == 0, col == pix - 1)

    def three(x):
        hi, mid = split2(x)
        lo = (x - hi.astype(jnp.float32) - mid.astype(jnp.float32)).astype(jnp.bfloat16)
        return hi, mid, lo

    loads[1].wait()
    one_hot = jnp.where(col == jnp.where(row < h, 2 * row, 2 * (row - h) + 1), 1.0, 0.0)
    one_hot_t = jnp.where(row == jnp.where(col < h, 2 * col, 2 * (col - h) + 1), 1.0, 0.0)
    ph, pt = one_hot.astype(jnp.bfloat16), one_hot_t.astype(jnp.bfloat16)
    half_done = sum(
        jnp.dot(ph, part, preferred_element_type=jnp.float32) for part in three(measured[...])
    )
    misfit[...] = -sum(
        jnp.dot(part, pt, preferred_element_type=jnp.float32) for part in three(half_done)
    )
    loads[0].wait()
    loads[2].wait()
    loads[3].wait()
    loads[4].wait()

    def probe_light(m, _):
        re0, im0 = probe[0, m], probe[1, m]
        sums[0, 0, body] += re0 * re0 + im0 * im0
        return 0

    lax.fori_loop(0, modes, probe_light, 0)

    pl.semaphore_wait(barrier, sum(there.astype(jnp.int32) for there, _ in neighbours))

    for s in range(2):

        @pl.when(up)
        def _():
            upward[s].start()

        @pl.when(left)
        def _():
            sideways[s].start()

    def get_window(s):
        @pl.when(down)
        def _():
            upward[s].wait_recv()

        @pl.when(down & left)
        def _():
            corners[s].start()

        @pl.when(right)
        def _():
            sideways[s].wait_recv()

        @pl.when(down & right)
        def _():
            corners[s].wait_recv()

        for p in range(2):
            rows = pltpu.roll(exts[s][p], up_roll, 0)[:pix]
            window = pltpu.roll(rows, left_roll, 1)[:, :pix]
            trans[2 * s + p] = window + 1.0 if p == 0 else window

    def first_slice(m, _):
        re0, im0 = probe[0, m], probe[1, m]
        tr, ti = trans[0], trans[1]
        re1, im1 = propagate(re0 * tr - im0 * ti, re0 * ti + im0 * tr, 1.0, edges)
        wave1[0, m] = re1
        wave1[1, m] = im1
        sums[0, 1, body] += re1 * re1 + im1 * im1
        return 0

    def second_slice(m, _):
        re1, im1 = wave1[0, m], wave1[1, m]
        tr, ti = trans[2], trans[3]
        er, ei = re1 * tr - im1 * ti, re1 * ti + im1 * tr
        even = right_dot(
            jnp.concatenate([er[:, :h] + er[:, h:], ei[:, :h] + ei[:, h:]], axis=1),
            tables[4], tables[5],
        )
        odd = right_dot(
            jnp.concatenate([er[:, :h] - er[:, h:], ei[:, :h] - ei[:, h:]], axis=1),
            tables[6], tables[7],
        )
        fr = jnp.concatenate([even[:, :h], odd[:, :h]], axis=1)
        fi = jnp.concatenate([even[:, h:], odd[:, h:]], axis=1)
        f_even = left_dot(
            tables[0], tables[1],
            jnp.concatenate([fr[:h] + fr[h:], fi[:h] + fi[h:]], axis=0),
        )
        f_odd = left_dot(
            tables[2], tables[3],
            jnp.concatenate([fr[:h] - fr[h:], fi[:h] - fi[h:]], axis=0),
        )
        far[0, m] = f_even
        far[1, m] = f_odd
        misfit[:h] += f_even[:h] * f_even[:h] + f_even[h:] * f_even[h:]
        misfit[h:] += f_odd[:h] * f_odd[:h] + f_odd[h:] * f_odd[h:]
        return 0

    def back_to_second(m, _):
        m_even, m_odd = 2.0 * misfit[:h], 2.0 * misfit[h:]
        b_even = left_dot(
            tables[4], tables[5], far[0, m] * jnp.concatenate([m_even, m_even], axis=0)
        )
        b_odd = left_dot(
            tables[6], tables[7], far[1, m] * jnp.concatenate([m_odd, m_odd], axis=0)
        )
        top, low = b_even + b_odd, b_even - b_odd
        br = jnp.concatenate([top[:h], low[:h]], axis=0)
        bi = jnp.concatenate([top[h:], low[h:]], axis=0)
        c_even = right_dot(
            jnp.concatenate([br[:, :h], bi[:, :h]], axis=1), tables[0], tables[1]
        )
        c_odd = right_dot(
            jnp.concatenate([br[:, h:], bi[:, h:]], axis=1), tables[2], tables[3]
        )
        lo, hi = c_even + c_odd, c_even - c_odd
        br = jnp.concatenate([lo[:, :h], hi[:, :h]], axis=1)
        bi = jnp.concatenate([lo[:, h:], hi[:, h:]], axis=1)
        wr, wi = wave1[0, m], wave1[1, m]
        sums[1, 0, body] += wr * br + wi * bi
        sums[1, 1, body] += wr * bi - wi * br
        tr, ti = trans[2], trans[3]
        far[0, m] = tr * br + ti * bi
        far[1, m] = tr * bi - ti * br
        return 0

    def back_to_first(m, _):
        br, bi = propagate(far[0, m], far[1, m], -1.0, edges)
        wr, wi = probe[0, m], probe[1, m]
        sums[2, 0, body] += wr * br + wi * bi
        sums[2, 1, body] += wr * bi - wi * br
        return 0

    to_right = [
        remote(ty_out.at[g], ty_in.at[g], r1_send.at[g], r1_recv.at[g], {"ty": ty_right})
        for g in range(3)
    ]
    to_below = [
        remote(work.at[g, :, beyond, :], tx_in.at[g], r2_send.at[g], r2_recv.at[g],
               {"tx": tx_down})
        for g in range(3)
    ]

    def place(g):
        for p in range(2):
            rows = pltpu.roll(sums[g, p], r, 0)
            spread = jnp.concatenate([rows, jnp.zeros((wide, rim), jnp.float32)], axis=1)
            spread = pltpu.roll(spread, c, 1)
            work[g, p] = spread[:, :side]
            ty_out[g, p] = spread[:, side:]

        @pl.when(right)
        def _():
            to_right[g].start()

    def add_sideways(g):
        @pl.when(left)
        def _():
            to_right[g].wait_recv()
            work[g, :, :, first] += ty_in[g]

        @pl.when(down)
        def _():
            to_below[g].start()

    def add_above(g):
        @pl.when(up)
        def _():
            to_below[g].wait_recv()
            work[g, :, first, :] += tx_in[g]

    share = rim // 2
    piece = share // PIECES

    def rows_of(k, way):
        block, q = k // PIECES, k % PIECES
        base = (rim, 0)[block] + q * piece
        return pl.ds(pl.multiple_of(base + (1 - way) * share, 8), piece)

    def sum_copy(g, k, way, target):
        rows = rows_of(k, way)
        return remote(
            work.at[g, :, rows, :], rs_in.at[g, :, rows, :],
            rs_send.at[g, k, way], rs_recv.at[g, k, way], {"scan": target})

    def new_copy(s, k, way, target):
        rows = rows_of(k, way)
        place = out.at[pl.ds(2 * s, 2), rows, :]
        return remote(
            place, place, ag_send.at[s, k, way], ag_recv.at[s, k, way], {"scan": target})

    def sum_near(g, k):
        @pl.when(outer)
        def _():
            rows = rows_of(k, near_way)
            sum_copy(g, k, near_way, inward).wait_recv()
            work[g, :, rows, :] += rs_in[g, :, rows, :]

        sum_copy(g, k, near_way, inward).start()

    def sum_far(g, k):
        rows = rows_of(k, far_way)
        sum_copy(g, k, far_way, outward).wait_recv()
        work[g, :, rows, :] += rs_in[g, :, rows, :]

        @pl.when(outer)
        def _():
            sum_copy(g, k, far_way, outward).start()

    def renew(s, k):
        g = 2 - s

        @pl.when(jnp.logical_not(outer))
        def _():
            rows = rows_of(k, far_way)
            light = work[0, s, rows, :] + 1.0
            for p in range(2):
                out[2 * s + p, rows, :] = (
                    exts[s][p, rows, near] - step_size * work[g, p, rows, :] / light
                )
            new_copy(s, k, far_way, inward).start()

    def new_near(s, k):
        @pl.when(outer)
        def _():
            new_copy(s, k, far_way, inward).wait_recv()
            new_copy(s, k, far_way, inward).start()

    def new_far(s, k):
        new_copy(s, k, near_way, outward).wait_recv()

        @pl.when(outer)
        def _():
            new_copy(s, k, near_way, outward).start()

    pieces = 2 * PIECES

    get_window(0)
    lax.fori_loop(0, modes, first_slice, 0, unroll=2)
    place(0)
    get_window(1)
    lax.fori_loop(0, modes // 2, second_slice, 0, unroll=2)
    add_sideways(0)
    lax.fori_loop(modes // 2, modes, second_slice, 0, unroll=2)
    add_above(0)
    for k in range(pieces):
        sum_near(0, k)
    lax.fori_loop(0, modes // 2, back_to_second, 0, unroll=2)
    for k in range(pieces):
        sum_far(0, k)
    lax.fori_loop(modes // 2, modes, back_to_second, 0, unroll=2)
    place(1)
    lax.fori_loop(0, modes // 2, back_to_first, 0, unroll=2)
    add_sideways(1)
    for k in range(PIECES):
        sum_near(1, k)
    lax.fori_loop(modes // 2, modes, back_to_first, 0, unroll=2)
    place(2)
    add_sideways(2)
    add_above(1)
    jobs = [(1, k) for k in range(pieces)] + [(2, k) for k in range(pieces)]
    for t in range(len(jobs) + 5):
        if PIECES <= t < len(jobs):
            if t == len(jobs) - PIECES:
                add_above(2)
            sum_near(*jobs[t])
        if 0 <= t - 2 < len(jobs):
            g, k = jobs[t - 2]
            sum_far(g, k)
            renew(2 - g, k)
        if 0 <= t - 4 < len(jobs):
            g, k = jobs[t - 4]
            new_near(2 - g, k)
        if 0 <= t - 5 < len(jobs):
            g, k = jobs[t - 5]
            new_far(2 - g, k)

    for s in range(2):

        @pl.when(up)
        def _():
            upward[s].wait_send()

        @pl.when(left)
        def _():
            sideways[s].wait_send()

        @pl.when(down & left)
        def _():
            corners[s].wait_send()

    for g in range(3):

        @pl.when(right)
        def _():
            to_right[g].wait_send()

        @pl.when(down)
        def _():
            to_below[g].wait_send()

        for k in range(pieces):
            sum_copy(g, k, near_way, inward).wait_send()

            @pl.when(outer)
            def _():
                sum_copy(g, k, far_way, outward).wait_send()

    for s in range(2):
        for k in range(pieces):
            new_copy(s, k, far_way, inward).wait_send()

            @pl.when(outer)
            def _():
                new_copy(s, k, near_way, outward).wait_send()


def on_device(n_scan, n_tx, n_ty, object_slices, probe_modes, corners, measured):
    layers, side = object_slices.shape[0], object_slices.shape[2]
    modes, pixels = probe_modes.shape[1], probe_modes.shape[-1]
    rim = pixels // 2
    wide = side + rim
    tables = jnp.asarray(dft_tables(pixels))
    tile = object_slices.reshape(2 * layers, side, side)
    anywhere = pl.BlockSpec(memory_space=pl.ANY)
    vmem, dma, f32 = pltpu.VMEM, pltpu.SemaphoreType.DMA, jnp.float32
    pieces = 2 * PIECES
    updated = pl.pallas_call(
        functools.partial(iteration_kernel, n_scan, n_tx, n_ty),
        out_shape=jax.ShapeDtypeStruct(tile.shape, f32),
        in_specs=[pl.BlockSpec(memory_space=pltpu.SMEM)] + [anywhere] * 4,
        out_specs=pl.BlockSpec(memory_space=pltpu.VMEM),
        scratch_shapes=[
            vmem((2, modes, pixels, pixels), f32),
            vmem((pixels, pixels), f32),
            vmem(tables.shape, tables.dtype),
            vmem((2, wide, wide), f32),
            vmem((2, wide, wide), f32),
            vmem((4, pixels, pixels), f32),
            vmem((2, modes, pixels, pixels), f32),
            vmem((2, modes, pixels, pixels), f32),
            vmem((pixels, pixels), f32),
            vmem((3, 2, wide, pixels), f32),
            vmem((3, 2, wide, side), f32),
            vmem((3, 2, wide, rim), f32),
            vmem((3, 2, wide, rim), f32),
            vmem((3, 2, rim, side), f32),
            vmem((3, 2, side, side), f32),
            dma((5,)), dma((2, 3)), dma((2, 3)), dma((3,)), dma((3,)), dma((3,)), dma((3,)),
            dma((3, pieces, 2)), dma((3, pieces, 2)), dma((2, pieces, 2)), dma((2, pieces, 2)),
        ],
        compiler_params=pltpu.CompilerParams(
            collective_id=0, has_side_effects=True, vmem_limit_bytes=60 * 1024 * 1024),
        name="iteration",
    )(corners[0, 0, 0], tile, probe_modes, measured[0, 0, 0], tables)
    return updated.reshape(object_slices.shape)


def solution(mesh):
    placed = (
        P(None, None, "tx", "ty"),
        P(),
        P("tx", "ty", "scan", None),
        P("tx", "ty", "scan", None, None),
    )
    sizes = (mesh.shape["scan"], mesh.shape["tx"], mesh.shape["ty"])
    return jax.shard_map(
        functools.partial(on_device, *sizes),
        mesh=mesh,
        in_specs=placed,
        out_specs=P(None, None, "tx", "ty"),
        check_vma=False,
    )
```

```python
import functools
import math

import jax
import jax.numpy as jnp
import numpy as np
from jax import lax
from jax.experimental import pallas as pl
from jax.experimental.pallas import tpu as pltpu
from jax.sharding import PartitionSpec as P

fresnel_coef = 0.1
step_size = 4.0
damping = 0.5 * fresnel_coef**2


def dft_tables(pixels):
    half = pixels // 2
    tables = []
    for parity in range(2):
        freq = 2 * np.arange(half) + parity
        angle = 2.0 * np.pi * ((freq[:, None] * np.arange(half)[None, :]) % pixels) / pixels
        c, s = np.cos(angle) / math.sqrt(pixels), np.sin(angle) / math.sqrt(pixels)
        tables.append(np.block([[c, s], [-s, c]]))
    tables += [t.T for t in tables]
    out = []
    for t in tables:
        t32 = t.astype(np.float32)
        high = t32.astype(jnp.bfloat16)
        low = (t - high.astype(np.float64)).astype(np.float32).astype(jnp.bfloat16)
        out += [high, low]
    return np.stack(out)


def split2(x):
    high = x.astype(jnp.bfloat16)
    return high, (x - high.astype(jnp.float32)).astype(jnp.bfloat16)


def right_dot(x, high, low):
    xh, xl = split2(x)
    lhs = jnp.concatenate([xh, xl, xh], axis=1)
    rhs = jnp.concatenate([high, high, low], axis=0)
    return jnp.dot(lhs, rhs, preferred_element_type=jnp.float32)


def left_dot(high, low, x):
    xh, xl = split2(x)
    lhs = jnp.concatenate([high, high, low], axis=1)
    rhs = jnp.concatenate([xh, xl, xh], axis=0)
    return jnp.dot(lhs, rhs, preferred_element_type=jnp.float32)


def propagate(re, im, sign, edges):
    first_row, last_row, first_col, last_col = edges
    n = re.shape[0]

    def lap(v):
        up = jnp.where(first_row, 0.0, pltpu.roll(v, 1, 0))
        down = jnp.where(last_row, 0.0, pltpu.roll(v, n - 1, 0))
        left = jnp.where(first_col, 0.0, pltpu.roll(v, 1, 1))
        right = jnp.where(last_col, 0.0, pltpu.roll(v, n - 1, 1))
        return (up + down) + (left + right) - 4.0 * v

    l_re, l_im = lap(re), lap(im)
    ll_re, ll_im = lap(l_re), lap(l_im)
    coef = sign * fresnel_coef
    return re - coef * l_im - damping * ll_re, im + coef * l_re - damping * ll_im


MESH = pl.DeviceIdType.MESH
PIECES = 2
HOP = 2


def iteration_kernel(
    n, n_tx, n_ty, corner, tile, probe_in, measured_in, tables_in, out,
    probe, measured, tables, ext0, ext1, trans, wave1, far, misfit, sums,
    work, ty_out, ty_in, tx_in, rs_in, cross_in,
    local_sem, rim_send, rim_recv, r1_send, r1_recv, r2_send, r2_recv,
    rs_send, rs_recv, cross_recv, ag_send, ag_recv,
):
    me, tx, ty = lax.axis_index("scan"), lax.axis_index("tx"), lax.axis_index("ty")
    modes, pix = probe.shape[1], probe.shape[2]
    h = pix // 2
    side, wide = tile.shape[1], ext0.shape[1]
    rim = wide - side
    up, left = tx > 0, ty > 0
    down, right = tx + 1 < n_tx, ty + 1 < n_ty
    tx_up, ty_left = jnp.maximum(tx - 1, 0), jnp.maximum(ty - 1, 0)
    tx_down, ty_right = jnp.minimum(tx + 1, n_tx - 1), jnp.minimum(ty + 1, n_ty - 1)
    on_low = 2 * me < n
    step = jnp.where(on_low, 1, -1)
    outer = jnp.where(on_low, me > 0, me < n - 1)
    inward = jnp.clip(me + step, 0, n - 1)
    outward = jnp.clip(me - step, 0, n - 1)
    owner = (me == n // 2 - 1) | (me == n // 2)
    own_half = jnp.where(on_low, 0, 1)
    other_half = 1 - own_half

    barrier = pltpu.get_barrier_semaphore()
    neighbours = [
        (up, {"tx": tx_up}), (down, {"tx": tx_down}),
        (left, {"ty": ty_left}), (right, {"ty": ty_right}),
        (outer, {"scan": outward}), (me >= 0, {"scan": inward}),
    ]
    for there, target in neighbours:

        @pl.when(there)
        def _():
            pl.semaphore_signal(barrier, inc=1, device_id=target, device_id_type=MESH)

    exts = (ext0, ext1)
    loads = [
        pltpu.make_async_copy(probe_in, probe, local_sem.at[0]),
        pltpu.make_async_copy(measured_in, measured, local_sem.at[1]),
        pltpu.make_async_copy(tables_in, tables, local_sem.at[2]),
        pltpu.make_async_copy(
            tile.at[pl.ds(0, 2)], ext0.at[:, pl.ds(0, side), pl.ds(0, side)], local_sem.at[3]),
        pltpu.make_async_copy(
            tile.at[pl.ds(2, 2)], ext1.at[:, pl.ds(0, side), pl.ds(0, side)], local_sem.at[4]),
    ]
    for load in loads:
        load.start()

    r, c = corner[0], corner[1]
    up_roll = jnp.where(r == 0, 0, wide - r)
    left_roll = jnp.where(c == 0, 0, wide - c)

    def remote(source, place, sends, recvs, target):
        return pltpu.make_async_remote_copy(
            src_ref=source, dst_ref=place, send_sem=sends, recv_sem=recvs,
            device_id=target, device_id_type=MESH,
        )

    near, beyond, first = pl.ds(0, side), pl.ds(side, rim), pl.ds(0, rim)
    sideways, upward, corners = [], [], []
    for s in range(2):
        part, ext = tile.at[pl.ds(2 * s, 2)], exts[s]
        sideways.append(remote(
            part.at[:, :, first], ext.at[:, near, beyond],
            rim_send.at[s, 0], rim_recv.at[s, 0], {"ty": ty_left}))
        upward.append(remote(
            part.at[:, first, :], ext.at[:, beyond, near],
            rim_send.at[s, 1], rim_recv.at[s, 1], {"tx": tx_up}))
        corners.append(remote(
            ext.at[:, beyond, first], ext.at[:, beyond, beyond],
            rim_send.at[s, 2], rim_recv.at[s, 2], {"ty": ty_left}))

    for s in range(2):
        ext = exts[s]

        @pl.when(jnp.logical_not(right))
        def _():
            ext[:, near, beyond] = jnp.zeros((2, side, rim), jnp.float32)

        @pl.when(jnp.logical_not(down))
        def _():
            ext[:, beyond, near] = jnp.zeros((2, rim, side), jnp.float32)

        @pl.when(jnp.logical_not(right & down))
        def _():
            ext[:, beyond, beyond] = jnp.zeros((2, rim, rim), jnp.float32)

    sums[...] = jnp.zeros_like(sums)
    body = pl.ds(0, pix)

    row = lax.broadcasted_iota(jnp.int32, (pix, pix), 0)
    col = lax.broadcasted_iota(jnp.int32, (pix, pix), 1)
    edges = (row == 0, row == pix - 1, col == 0, col == pix - 1)

    def three(x):
        hi, mid = split2(x)
        lo = (x - hi.astype(jnp.float32) - mid.astype(jnp.float32)).astype(jnp.bfloat16)
        return hi, mid, lo

    loads[1].wait()
    one_hot = jnp.where(col == jnp.where(row < h, 2 * row, 2 * (row - h) + 1), 1.0, 0.0)
    one_hot_t = jnp.where(row == jnp.where(col < h, 2 * col, 2 * (col - h) + 1), 1.0, 0.0)
    ph, pt = one_hot.astype(jnp.bfloat16), one_hot_t.astype(jnp.bfloat16)
    half_done = sum(
        jnp.dot(ph, part, preferred_element_type=jnp.float32) for part in three(measured[...])
    )
    misfit[...] = -sum(
        jnp.dot(part, pt, preferred_element_type=jnp.float32) for part in three(half_done)
    )
    loads[0].wait()
    loads[2].wait()
    loads[3].wait()
    loads[4].wait()

    def probe_light(m, _):
        re0, im0 = probe[0, m], probe[1, m]
        sums[0, 0, body] += re0 * re0 + im0 * im0
        return 0

    lax.fori_loop(0, modes, probe_light, 0)

    pl.semaphore_wait(barrier, sum(there.astype(jnp.int32) for there, _ in neighbours))

    for s in range(2):

        @pl.when(up)
        def _():
            upward[s].start()

        @pl.when(left)
        def _():
            sideways[s].start()

    def get_window(s):
        @pl.when(down)
        def _():
            upward[s].wait_recv()

        @pl.when(down & left)
        def _():
            corners[s].start()

        @pl.when(right)
        def _():
            sideways[s].wait_recv()

        @pl.when(down & right)
        def _():
            corners[s].wait_recv()

        for p in range(2):
            rows = pltpu.roll(exts[s][p], up_roll, 0)[:pix]
            window = pltpu.roll(rows, left_roll, 1)[:, :pix]
            trans[2 * s + p] = window + 1.0 if p == 0 else window

    def first_slice(m, _):
        re0, im0 = probe[0, m], probe[1, m]
        tr, ti = trans[0], trans[1]
        re1, im1 = propagate(re0 * tr - im0 * ti, re0 * ti + im0 * tr, 1.0, edges)
        wave1[0, m] = re1
        wave1[1, m] = im1
        sums[0, 1, body] += re1 * re1 + im1 * im1
        return 0

    def second_slice(m, _):
        re1, im1 = wave1[0, m], wave1[1, m]
        tr, ti = trans[2], trans[3]
        er, ei = re1 * tr - im1 * ti, re1 * ti + im1 * tr
        even = right_dot(
            jnp.concatenate([er[:, :h] + er[:, h:], ei[:, :h] + ei[:, h:]], axis=1),
            tables[4], tables[5],
        )
        odd = right_dot(
            jnp.concatenate([er[:, :h] - er[:, h:], ei[:, :h] - ei[:, h:]], axis=1),
            tables[6], tables[7],
        )
        fr = jnp.concatenate([even[:, :h], odd[:, :h]], axis=1)
        fi = jnp.concatenate([even[:, h:], odd[:, h:]], axis=1)
        f_even = left_dot(
            tables[0], tables[1],
            jnp.concatenate([fr[:h] + fr[h:], fi[:h] + fi[h:]], axis=0),
        )
        f_odd = left_dot(
            tables[2], tables[3],
            jnp.concatenate([fr[:h] - fr[h:], fi[:h] - fi[h:]], axis=0),
        )
        far[0, m] = f_even
        far[1, m] = f_odd
        misfit[:h] += f_even[:h] * f_even[:h] + f_even[h:] * f_even[h:]
        misfit[h:] += f_odd[:h] * f_odd[:h] + f_odd[h:] * f_odd[h:]
        return 0

    def back_to_second(m, _):
        m_even, m_odd = 2.0 * misfit[:h], 2.0 * misfit[h:]
        b_even = left_dot(
            tables[4], tables[5], far[0, m] * jnp.concatenate([m_even, m_even], axis=0)
        )
        b_odd = left_dot(
            tables[6], tables[7], far[1, m] * jnp.concatenate([m_odd, m_odd], axis=0)
        )
        top, low = b_even + b_odd, b_even - b_odd
        br = jnp.concatenate([top[:h], low[:h]], axis=0)
        bi = jnp.concatenate([top[h:], low[h:]], axis=0)
        c_even = right_dot(
            jnp.concatenate([br[:, :h], bi[:, :h]], axis=1), tables[0], tables[1]
        )
        c_odd = right_dot(
            jnp.concatenate([br[:, h:], bi[:, h:]], axis=1), tables[2], tables[3]
        )
        lo, hi = c_even + c_odd, c_even - c_odd
        br = jnp.concatenate([lo[:, :h], hi[:, :h]], axis=1)
        bi = jnp.concatenate([lo[:, h:], hi[:, h:]], axis=1)
        wr, wi = wave1[0, m], wave1[1, m]
        sums[1, 0, body] += wr * br + wi * bi
        sums[1, 1, body] += wr * bi - wi * br
        tr, ti = trans[2], trans[3]
        far[0, m] = tr * br + ti * bi
        far[1, m] = tr * bi - ti * br
        return 0

    def back_to_first(m, _):
        br, bi = propagate(far[0, m], far[1, m], -1.0, edges)
        wr, wi = probe[0, m], probe[1, m]
        sums[2, 0, body] += wr * br + wi * bi
        sums[2, 1, body] += wr * bi - wi * br
        return 0

    to_right = [
        remote(ty_out.at[g], ty_in.at[g], r1_send.at[g], r1_recv.at[g], {"ty": ty_right})
        for g in range(3)
    ]
    to_below = [
        remote(work.at[g, :, beyond, :], tx_in.at[g], r2_send.at[g], r2_recv.at[g],
               {"tx": tx_down})
        for g in range(3)
    ]

    def place(g):
        for p in range(2):
            rows = pltpu.roll(sums[g, p], r, 0)
            spread = jnp.concatenate([rows, jnp.zeros((wide, rim), jnp.float32)], axis=1)
            spread = pltpu.roll(spread, c, 1)
            work[g, p] = spread[:, :side]
            ty_out[g, p] = spread[:, side:]

        @pl.when(right)
        def _():
            to_right[g].start()

    def add_sideways(g):
        @pl.when(left)
        def _():
            to_right[g].wait_recv()
            work[g, :, :, first] += ty_in[g]

        @pl.when(down)
        def _():
            to_below[g].start()

    def add_above(g):
        @pl.when(up)
        def _():
            to_below[g].wait_recv()
            work[g, :, first, :] += tx_in[g]

    share = rim // 2
    piece = share // PIECES

    def rows_of(k, half):
        block, q = k // PIECES, k % PIECES
        base = (rim, 0)[block] + q * piece
        return pl.ds(pl.multiple_of(base + half * share, 8), piece)

    def sum_copy(g, k, half):
        rows = rows_of(k, half)
        return remote(
            work.at[g, :, rows, :], rs_in.at[g, :, rows, :],
            rs_send.at[g, k, half], rs_recv.at[g, k, half], {"scan": inward})

    def cross_copy(g, k, half):
        rows = rows_of(k, half)
        return remote(
            work.at[g, :, rows, :], cross_in.at[g, :, rows, :],
            rs_send.at[g, k, half], cross_recv.at[g, k], {"scan": inward})

    def new_copy(s, k, half, way):
        place = out.at[pl.ds(2 * s, 2), rows_of(k, half), :]
        return remote(
            place, place, ag_send.at[s, k, half, way], ag_recv.at[s, k, half],
            {"scan": (inward, outward)[way]})

    def add_outer(g, k, half):
        @pl.when(outer)
        def _():
            rows = rows_of(k, half)
            sum_copy(g, k, half).wait_recv()
            work[g, :, rows, :] += rs_in[g, :, rows, :]

    def pass_on(g, k):
        for half in (other_half, own_half):
            add_outer(g, k, half)
            sum_copy(g, k, half).start()

    def give(g, k):
        add_outer(g, k, other_half)
        cross_copy(g, k, other_half).start()

    def keep(g, k):
        add_outer(g, k, own_half)

    def total(g, k):
        rows = rows_of(k, own_half)
        cross_copy(g, k, own_half).wait_recv()
        work[g, :, rows, :] += cross_in[g, :, rows, :]

    def renew(g, k):
        s = 2 - g
        rows = rows_of(k, own_half)
        cross_copy(g, k, own_half).wait_recv()
        light = work[0, s, rows, :] + 1.0
        for p in range(2):
            grad = work[g, p, rows, :] + cross_in[g, p, rows, :]
            out[2 * s + p, rows, :] = exts[s][p, rows, near] - step_size * grad / light
        new_copy(s, k, own_half, 0).start()

        @pl.when(outer)
        def _():
            new_copy(s, k, own_half, 1).start()

    def spread(g, k, half):
        new_copy(2 - g, k, half, 1).wait_recv()

        @pl.when(outer)
        def _():
            new_copy(2 - g, k, half, 1).start()

    def spread_other(g, k):
        spread(g, k, other_half)

    def spread_both(g, k):
        spread(g, k, own_half)
        spread(g, k, other_half)

    def in_order(events):
        for _, _, action, arguments in sorted(events, key=lambda e: e[:2]):
            action(*arguments)

    def by_role(others, owners):
        if others:

            @pl.when(jnp.logical_not(owner))
            def _():
                in_order(others)

        if owners:

            @pl.when(owner)
            def _():
                in_order(owners)

    pieces = 2 * PIECES
    high, lower = range(PIECES), range(PIECES, pieces)
    every = range(pieces)

    def listed(action, g, ks, when=0):
        return [(when, i, action, (g, k)) for i, k in enumerate(ks)]

    get_window(0)
    lax.fori_loop(0, modes, first_slice, 0, unroll=2)
    place(0)
    get_window(1)
    lax.fori_loop(0, modes // 2, second_slice, 0, unroll=2)
    add_sideways(0)
    by_role(listed(pass_on, 0, high), [])
    lax.fori_loop(modes // 2, modes, second_slice, 0, unroll=2)
    add_above(0)
    by_role(listed(pass_on, 0, lower), listed(give, 0, high))
    lax.fori_loop(0, modes // 2, back_to_second, 0, unroll=2)
    by_role([], listed(give, 0, lower) + listed(keep, 0, every, 1))
    lax.fori_loop(modes // 2, modes, back_to_second, 0, unroll=2)
    place(1)
    by_role([], listed(total, 0, every))
    lax.fori_loop(0, modes // 8, back_to_first, 0)
    add_sideways(1)
    by_role(listed(pass_on, 1, high), [])
    lax.fori_loop(modes // 8, modes // 2, back_to_first, 0)
    lax.fori_loop(modes // 2, modes - modes // 4, back_to_first, 0, unroll=2)
    by_role([], listed(give, 1, high))
    lax.fori_loop(modes - modes // 4, modes, back_to_first, 0, unroll=2)
    place(2)
    both = [[], []]

    def plan(when, order, action, *arguments, who=(0, 1)):
        for role in who:
            both[role].append((when, order, action, arguments))

    plan(0, -1, add_sideways, 2)
    plan(0, -1, add_above, 1)
    plan(2 * PIECES, -1, add_above, 2)
    starts = [-3 * PIECES + 2 * k for k in high] + [2 * k for k in high]
    starts += [2 * PIECES + 2 * k for k in every]
    jobs = [(1, k) for k in every] + [(2, k) for k in every]
    for start, (g, k) in zip(starts, jobs):
        if (g, k) not in [(1, k) for k in high]:
            plan(start, 0, pass_on, g, k, who=(0,))
            plan(start + 1 + HOP, 1, give, g, k, who=(1,))
        plan(start + 2 + HOP, 2, keep, g, k, who=(1,))
        plan(start + 2 + 2 * HOP, 3, renew, g, k, who=(1,))
        plan(start + 3 + 3 * HOP, 4, spread_other, g, k, who=(1,))
        plan(start + 4 + 4 * HOP, 5, spread_both, g, k, who=(0,))
    by_role(*both)

    for s in range(2):

        @pl.when(up)
        def _():
            upward[s].wait_send()

        @pl.when(left)
        def _():
            sideways[s].wait_send()

        @pl.when(down & left)
        def _():
            corners[s].wait_send()

    for g in range(3):

        @pl.when(right)
        def _():
            to_right[g].wait_send()

        @pl.when(down)
        def _():
            to_below[g].wait_send()

        for k in every:
            sum_copy(g, k, other_half).wait_send()

            @pl.when(jnp.logical_not(owner))
            def _():
                sum_copy(g, k, own_half).wait_send()

    for s in range(2):
        for k in every:

            @pl.when(owner)
            def _():
                new_copy(s, k, own_half, 0).wait_send()

            @pl.when(outer)
            def _():
                new_copy(s, k, own_half, 1).wait_send()
                new_copy(s, k, other_half, 1).wait_send()


def on_device(n_scan, n_tx, n_ty, object_slices, probe_modes, corners, measured):
    layers, side = object_slices.shape[0], object_slices.shape[2]
    modes, pixels = probe_modes.shape[1], probe_modes.shape[-1]
    rim = pixels // 2
    wide = side + rim
    tables = jnp.asarray(dft_tables(pixels))
    tile = object_slices.reshape(2 * layers, side, side)
    anywhere = pl.BlockSpec(memory_space=pl.ANY)
    vmem, dma, f32 = pltpu.VMEM, pltpu.SemaphoreType.DMA, jnp.float32
    pieces = 2 * PIECES
    updated = pl.pallas_call(
        functools.partial(iteration_kernel, n_scan, n_tx, n_ty),
        out_shape=jax.ShapeDtypeStruct(tile.shape, f32),
        in_specs=[pl.BlockSpec(memory_space=pltpu.SMEM)] + [anywhere] * 4,
        out_specs=pl.BlockSpec(memory_space=pltpu.VMEM),
        scratch_shapes=[
            vmem((2, modes, pixels, pixels), f32),
            vmem((pixels, pixels), f32),
            vmem(tables.shape, tables.dtype),
            vmem((2, wide, wide), f32),
            vmem((2, wide, wide), f32),
            vmem((4, pixels, pixels), f32),
            vmem((2, modes, pixels, pixels), f32),
            vmem((2, modes, pixels, pixels), f32),
            vmem((pixels, pixels), f32),
            vmem((3, 2, wide, pixels), f32),
            vmem((3, 2, wide, side), f32),
            vmem((3, 2, wide, rim), f32),
            vmem((3, 2, wide, rim), f32),
            vmem((3, 2, rim, side), f32),
            vmem((3, 2, side, side), f32),
            vmem((3, 2, side, side), f32),
            dma((5,)), dma((2, 3)), dma((2, 3)), dma((3,)), dma((3,)), dma((3,)), dma((3,)),
            dma((3, pieces, 2)), dma((3, pieces, 2)), dma((3, pieces)),
            dma((2, pieces, 2, 2)), dma((2, pieces, 2)),
        ],
        compiler_params=pltpu.CompilerParams(
            collective_id=0, has_side_effects=True, vmem_limit_bytes=60 * 1024 * 1024),
        name="iteration",
    )(corners[0, 0, 0], tile, probe_modes, measured[0, 0, 0], tables)
    return updated.reshape(object_slices.shape)


def solution(mesh):
    placed = (
        P(None, None, "tx", "ty"),
        P(),
        P("tx", "ty", "scan", None),
        P("tx", "ty", "scan", None, None),
    )
    sizes = (mesh.shape["scan"], mesh.shape["tx"], mesh.shape["ty"])
    return jax.shard_map(
        functools.partial(on_device, *sizes),
        mesh=mesh,
        in_specs=placed,
        out_specs=P(None, None, "tx", "ty"),
        check_vma=False,
    )
```

```python
import functools
import math

import jax
import jax.numpy as jnp
import numpy as np
from jax import lax
from jax.experimental import pallas as pl
from jax.experimental.pallas import tpu as pltpu
from jax.sharding import PartitionSpec as P

fresnel_coef = 0.1
step_size = 4.0
damping = 0.5 * fresnel_coef**2


def dft_tables(pixels):
    half = pixels // 2
    tables = []
    for parity in range(2):
        freq = 2 * np.arange(half) + parity
        angle = 2.0 * np.pi * ((freq[:, None] * np.arange(half)[None, :]) % pixels) / pixels
        c, s = np.cos(angle) / math.sqrt(pixels), np.sin(angle) / math.sqrt(pixels)
        tables.append(np.block([[c, s], [-s, c]]))
    tables += [t.T for t in tables]
    out = []
    for t in tables:
        t32 = t.astype(np.float32)
        high = t32.astype(jnp.bfloat16)
        low = (t - high.astype(np.float64)).astype(np.float32).astype(jnp.bfloat16)
        out += [high, low]
    return np.stack(out)


def split2(x):
    high = x.astype(jnp.bfloat16)
    return high, (x - high.astype(jnp.float32)).astype(jnp.bfloat16)


def right_dot(x, high, low):
    xh, xl = split2(x)
    lhs = jnp.concatenate([xh, xl, xh], axis=1)
    rhs = jnp.concatenate([high, high, low], axis=0)
    return jnp.dot(lhs, rhs, preferred_element_type=jnp.float32)


def left_dot(high, low, x):
    xh, xl = split2(x)
    lhs = jnp.concatenate([high, high, low], axis=1)
    rhs = jnp.concatenate([xh, xl, xh], axis=0)
    return jnp.dot(lhs, rhs, preferred_element_type=jnp.float32)


def propagate(re, im, sign, edges):
    first_row, last_row, first_col, last_col = edges
    n = re.shape[0]

    def lap(v):
        up = jnp.where(first_row, 0.0, pltpu.roll(v, 1, 0))
        down = jnp.where(last_row, 0.0, pltpu.roll(v, n - 1, 0))
        left = jnp.where(first_col, 0.0, pltpu.roll(v, 1, 1))
        right = jnp.where(last_col, 0.0, pltpu.roll(v, n - 1, 1))
        return (up + down) + (left + right) - 4.0 * v

    l_re, l_im = lap(re), lap(im)
    ll_re, ll_im = lap(l_re), lap(l_im)
    coef = sign * fresnel_coef
    return re - coef * l_im - damping * ll_re, im + coef * l_re - damping * ll_im


MESH = pl.DeviceIdType.MESH
PIECES = 2
HOP = 2
UNROLL = 4


def iteration_kernel(
    n, n_tx, n_ty, corner, tile, probe_in, measured_in, tables_in, out,
    probe, measured, tables, ext0, ext1, trans, wave1, far, misfit, sums,
    work, ty_out, ty_in, tx_in, rs_in, cross_in,
    local_sem, rim_send, rim_recv, r1_send, r1_recv, r2_send, r2_recv,
    rs_send, rs_recv, cross_recv, ag_send, ag_recv,
):
    me, tx, ty = lax.axis_index("scan"), lax.axis_index("tx"), lax.axis_index("ty")
    modes, pix = probe.shape[1], probe.shape[2]
    h = pix // 2
    side, wide = tile.shape[1], ext0.shape[1]
    rim = wide - side
    up, left = tx > 0, ty > 0
    down, right = tx + 1 < n_tx, ty + 1 < n_ty
    tx_up, ty_left = jnp.maximum(tx - 1, 0), jnp.maximum(ty - 1, 0)
    tx_down, ty_right = jnp.minimum(tx + 1, n_tx - 1), jnp.minimum(ty + 1, n_ty - 1)
    on_low = 2 * me < n
    step = jnp.where(on_low, 1, -1)
    outer = jnp.where(on_low, me > 0, me < n - 1)
    inward = jnp.clip(me + step, 0, n - 1)
    outward = jnp.clip(me - step, 0, n - 1)
    owner = (me == n // 2 - 1) | (me == n // 2)
    own_half = jnp.where(on_low, 0, 1)
    other_half = 1 - own_half

    barrier = pltpu.get_barrier_semaphore()
    neighbours = [
        (up, {"tx": tx_up}), (down, {"tx": tx_down}),
        (left, {"ty": ty_left}), (right, {"ty": ty_right}),
        (outer, {"scan": outward}), (me >= 0, {"scan": inward}),
    ]
    for there, target in neighbours:

        @pl.when(there)
        def _():
            pl.semaphore_signal(barrier, inc=1, device_id=target, device_id_type=MESH)

    exts = (ext0, ext1)
    loads = [
        pltpu.make_async_copy(probe_in, probe, local_sem.at[0]),
        pltpu.make_async_copy(measured_in, measured, local_sem.at[1]),
        pltpu.make_async_copy(tables_in, tables, local_sem.at[2]),
        pltpu.make_async_copy(
            tile.at[pl.ds(0, 2)], ext0.at[:, pl.ds(0, side), pl.ds(0, side)], local_sem.at[3]),
        pltpu.make_async_copy(
            tile.at[pl.ds(2, 2)], ext1.at[:, pl.ds(0, side), pl.ds(0, side)], local_sem.at[4]),
    ]
    for load in loads:
        load.start()

    r, c = corner[0], corner[1]
    up_roll = jnp.where(r == 0, 0, wide - r)
    left_roll = jnp.where(c == 0, 0, wide - c)

    def remote(source, place, sends, recvs, target):
        return pltpu.make_async_remote_copy(
            src_ref=source, dst_ref=place, send_sem=sends, recv_sem=recvs,
            device_id=target, device_id_type=MESH,
        )

    near, beyond, first = pl.ds(0, side), pl.ds(side, rim), pl.ds(0, rim)
    sideways, upward, corners = [], [], []
    for s in range(2):
        part, ext = tile.at[pl.ds(2 * s, 2)], exts[s]
        sideways.append(remote(
            part.at[:, :, first], ext.at[:, near, beyond],
            rim_send.at[s, 0], rim_recv.at[s, 0], {"ty": ty_left}))
        upward.append(remote(
            part.at[:, first, :], ext.at[:, beyond, near],
            rim_send.at[s, 1], rim_recv.at[s, 1], {"tx": tx_up}))
        corners.append(remote(
            ext.at[:, beyond, first], ext.at[:, beyond, beyond],
            rim_send.at[s, 2], rim_recv.at[s, 2], {"ty": ty_left}))

    for s in range(2):
        ext = exts[s]

        @pl.when(jnp.logical_not(right))
        def _():
            ext[:, near, beyond] = jnp.zeros((2, side, rim), jnp.float32)

        @pl.when(jnp.logical_not(down))
        def _():
            ext[:, beyond, near] = jnp.zeros((2, rim, side), jnp.float32)

        @pl.when(jnp.logical_not(right & down))
        def _():
            ext[:, beyond, beyond] = jnp.zeros((2, rim, rim), jnp.float32)

    sums[...] = jnp.zeros_like(sums)
    body = pl.ds(0, pix)

    row = lax.broadcasted_iota(jnp.int32, (pix, pix), 0)
    col = lax.broadcasted_iota(jnp.int32, (pix, pix), 1)
    edges = (row == 0, row == pix - 1, col == 0, col == pix - 1)

    def three(x):
        hi, mid = split2(x)
        lo = (x - hi.astype(jnp.float32) - mid.astype(jnp.float32)).astype(jnp.bfloat16)
        return hi, mid, lo

    loads[1].wait()
    one_hot = jnp.where(col == jnp.where(row < h, 2 * row, 2 * (row - h) + 1), 1.0, 0.0)
    one_hot_t = jnp.where(row == jnp.where(col < h, 2 * col, 2 * (col - h) + 1), 1.0, 0.0)
    ph, pt = one_hot.astype(jnp.bfloat16), one_hot_t.astype(jnp.bfloat16)
    half_done = sum(
        jnp.dot(ph, part, preferred_element_type=jnp.float32) for part in three(measured[...])
    )
    misfit[...] = -sum(
        jnp.dot(part, pt, preferred_element_type=jnp.float32) for part in three(half_done)
    )
    loads[0].wait()
    loads[2].wait()
    loads[3].wait()
    loads[4].wait()

    def probe_light(m, _):
        re0, im0 = probe[0, m], probe[1, m]
        sums[0, 0, body] += re0 * re0 + im0 * im0
        return 0

    lax.fori_loop(0, modes, probe_light, 0)

    pl.semaphore_wait(barrier, sum(there.astype(jnp.int32) for there, _ in neighbours))

    for s in range(2):

        @pl.when(up)
        def _():
            upward[s].start()

        @pl.when(left)
        def _():
            sideways[s].start()

    def get_window(s):
        @pl.when(down)
        def _():
            upward[s].wait_recv()

        @pl.when(down & left)
        def _():
            corners[s].start()

        @pl.when(right)
        def _():
            sideways[s].wait_recv()

        @pl.when(down & right)
        def _():
            corners[s].wait_recv()

        for p in range(2):
            rows = pltpu.roll(exts[s][p], up_roll, 0)[:pix]
            window = pltpu.roll(rows, left_roll, 1)[:, :pix]
            trans[2 * s + p] = window + 1.0 if p == 0 else window

    def first_slice(m, _):
        re0, im0 = probe[0, m], probe[1, m]
        tr, ti = trans[0], trans[1]
        re1, im1 = propagate(re0 * tr - im0 * ti, re0 * ti + im0 * tr, 1.0, edges)
        wave1[0, m] = re1
        wave1[1, m] = im1
        sums[0, 1, body] += re1 * re1 + im1 * im1
        return 0

    def second_slice(m, _):
        re1, im1 = wave1[0, m], wave1[1, m]
        tr, ti = trans[2], trans[3]
        er, ei = re1 * tr - im1 * ti, re1 * ti + im1 * tr
        even = right_dot(
            jnp.concatenate([er[:, :h] + er[:, h:], ei[:, :h] + ei[:, h:]], axis=1),
            tables[4], tables[5],
        )
        odd = right_dot(
            jnp.concatenate([er[:, :h] - er[:, h:], ei[:, :h] - ei[:, h:]], axis=1),
            tables[6], tables[7],
        )
        fr = jnp.concatenate([even[:, :h], odd[:, :h]], axis=1)
        fi = jnp.concatenate([even[:, h:], odd[:, h:]], axis=1)
        f_even = left_dot(
            tables[0], tables[1],
            jnp.concatenate([fr[:h] + fr[h:], fi[:h] + fi[h:]], axis=0),
        )
        f_odd = left_dot(
            tables[2], tables[3],
            jnp.concatenate([fr[:h] - fr[h:], fi[:h] - fi[h:]], axis=0),
        )
        far[0, m] = f_even
        far[1, m] = f_odd
        misfit[:h] += f_even[:h] * f_even[:h] + f_even[h:] * f_even[h:]
        misfit[h:] += f_odd[:h] * f_odd[:h] + f_odd[h:] * f_odd[h:]
        return 0

    def back_to_second(m, _):
        m_even, m_odd = 2.0 * misfit[:h], 2.0 * misfit[h:]
        b_even = left_dot(
            tables[4], tables[5], far[0, m] * jnp.concatenate([m_even, m_even], axis=0)
        )
        b_odd = left_dot(
            tables[6], tables[7], far[1, m] * jnp.concatenate([m_odd, m_odd], axis=0)
        )
        top, low = b_even + b_odd, b_even - b_odd
        br = jnp.concatenate([top[:h], low[:h]], axis=0)
        bi = jnp.concatenate([top[h:], low[h:]], axis=0)
        c_even = right_dot(
            jnp.concatenate([br[:, :h], bi[:, :h]], axis=1), tables[0], tables[1]
        )
        c_odd = right_dot(
            jnp.concatenate([br[:, h:], bi[:, h:]], axis=1), tables[2], tables[3]
        )
        lo, hi = c_even + c_odd, c_even - c_odd
        br = jnp.concatenate([lo[:, :h], hi[:, :h]], axis=1)
        bi = jnp.concatenate([lo[:, h:], hi[:, h:]], axis=1)
        wr, wi = wave1[0, m], wave1[1, m]
        sums[1, 0, body] += wr * br + wi * bi
        sums[1, 1, body] += wr * bi - wi * br
        tr, ti = trans[2], trans[3]
        far[0, m] = tr * br + ti * bi
        far[1, m] = tr * bi - ti * br
        return 0

    def back_to_first(m, _):
        br, bi = propagate(far[0, m], far[1, m], -1.0, edges)
        wr, wi = probe[0, m], probe[1, m]
        sums[2, 0, body] += wr * br + wi * bi
        sums[2, 1, body] += wr * bi - wi * br
        return 0

    def planes(g):
        return (0, pl.ds(g, 1)) if g < 2 else (g - 1, pl.ds(0, 2))

    to_right = [
        remote(ty_out.at[planes(g)], ty_in.at[planes(g)], r1_send.at[g], r1_recv.at[g],
               {"ty": ty_right})
        for g in range(4)
    ]
    to_below = [
        remote(work.at[planes(g)].at[:, beyond, :], tx_in.at[planes(g)], r2_send.at[g],
               r2_recv.at[g], {"tx": tx_down})
        for g in range(4)
    ]

    def place(g):
        group, which = planes(g)
        for p in range(which.start, which.start + which.size):
            rows = pltpu.roll(sums[group, p], r, 0)
            spread = jnp.concatenate([rows, jnp.zeros((wide, rim), jnp.float32)], axis=1)
            spread = pltpu.roll(spread, c, 1)
            work[group, p] = spread[:, :side]
            ty_out[group, p] = spread[:, side:]

        @pl.when(right)
        def _():
            to_right[g].start()

    def add_sideways(g):
        group, which = planes(g)

        @pl.when(left)
        def _():
            to_right[g].wait_recv()
            work[group, which, :, first] += ty_in[group, which]

    def go_below(g):
        @pl.when(down)
        def _():
            to_below[g].start()

    def add_above(g):
        group, which = planes(g)

        @pl.when(up)
        def _():
            to_below[g].wait_recv()
            work[group, which, first, :] += tx_in[group, which]

    share = rim // 2
    piece = share // PIECES

    def rows_of(k, half):
        block, q = k // PIECES, k % PIECES
        base = (rim, 0)[block] + q * piece
        return pl.ds(pl.multiple_of(base + half * share, 8), piece)

    def part(ref, g, rows):
        group, which = planes(g)
        return ref.at[group, which, rows, :]

    def sum_copy(g, k, half):
        rows = rows_of(k, half)
        return remote(
            part(work, g, rows), part(rs_in, g, rows),
            rs_send.at[g, k, half], rs_recv.at[g, k, half], {"scan": inward})

    def cross_copy(g, k, half):
        rows = rows_of(k, half)
        return remote(
            part(work, g, rows), part(cross_in, g, rows),
            rs_send.at[g, k, half], cross_recv.at[g, k], {"scan": inward})

    def new_copy(g, k, half, way):
        place = out.at[pl.ds(2 * (3 - g), 2), rows_of(k, half), :]
        return remote(
            place, place, ag_send.at[g - 2, k, half, way], ag_recv.at[g - 2, k, half],
            {"scan": (inward, outward)[way]})

    def add_outer(g, k, half):
        @pl.when(outer)
        def _():
            rows = rows_of(k, half)
            sum_copy(g, k, half).wait_recv()
            part(work, g, rows)[...] += part(rs_in, g, rows)[...]

    def pass_half(g, k, half):
        add_outer(g, k, half)
        sum_copy(g, k, half).start()

    def pass_on(g, k):
        pass_half(g, k, other_half)
        pass_half(g, k, own_half)

    def give(g, k):
        add_outer(g, k, other_half)
        cross_copy(g, k, other_half).start()

    def keep(g, k):
        add_outer(g, k, own_half)

    def total(g, k):
        rows = rows_of(k, own_half)
        cross_copy(g, k, own_half).wait_recv()
        part(work, g, rows)[...] += part(cross_in, g, rows)[...]

    def renew(g, k):
        s = 3 - g
        rows = rows_of(k, own_half)
        cross_copy(g, k, own_half).wait_recv()
        light = work[0, s, rows, :] + 1.0
        for p in range(2):
            grad = work[g - 1, p, rows, :] + cross_in[g - 1, p, rows, :]
            out[2 * s + p, rows, :] = exts[s][p, rows, near] - step_size * grad / light
        new_copy(g, k, own_half, 0).start()

        @pl.when(outer)
        def _():
            new_copy(g, k, own_half, 1).start()

    def spread(g, k, half):
        new_copy(g, k, half, 1).wait_recv()

        @pl.when(outer)
        def _():
            new_copy(g, k, half, 1).start()

    def spread_other(g, k):
        spread(g, k, other_half)

    def spread_both(g, k):
        spread(g, k, own_half)
        spread(g, k, other_half)

    def in_order(events):
        for _, _, action, arguments in sorted(events, key=lambda e: e[:2]):
            action(*arguments)

    def by_role(others, owners):
        if others:

            @pl.when(jnp.logical_not(owner))
            def _():
                in_order(others)

        if owners:

            @pl.when(owner)
            def _():
                in_order(owners)

    pieces = 2 * PIECES
    high, lower = range(PIECES), range(PIECES, pieces)
    every = range(pieces)

    def listed(action, g, ks, when=0):
        return [(when, i, action, (g, k)) for i, k in enumerate(ks)]

    place(0)
    add_sideways(0)
    by_role(listed(pass_on, 0, high), [])
    get_window(0)
    lax.fori_loop(0, modes, first_slice, 0, unroll=4)
    place(1)
    get_window(1)
    add_sideways(1)
    go_below(0)
    go_below(1)
    by_role(listed(pass_on, 1, high), listed(give, 0, high))
    lax.fori_loop(0, modes, second_slice, 0, unroll=8)
    add_above(0)
    add_above(1)
    by_role(listed(pass_on, 0, lower) + listed(pass_on, 1, lower), listed(give, 1, high))
    lax.fori_loop(0, modes, back_to_second, 0, unroll=8)
    place(2)
    add_sideways(2)
    go_below(2)
    by_role(listed(pass_on, 2, high), [])
    lax.fori_loop(0, modes // 2, back_to_first, 0, unroll=UNROLL)
    by_role([], listed(give, 0, lower) + listed(give, 1, lower, 1) + listed(keep, 0, every, 2)
            + listed(keep, 1, every, 2) + listed(give, 2, high, 3))
    lax.fori_loop(modes // 2, modes, back_to_first, 0, unroll=UNROLL)
    place(3)
    both = [[], []]

    def plan(when, order, action, *arguments, who=(0, 1)):
        for role in who:
            both[role].append((when, order, action, arguments))

    plan(0, -2, add_sideways, 3)
    plan(0, -2, go_below, 3)
    plan(0, -1, add_above, 2)
    for g in (0, 1):
        for k in every:
            plan(0, -0.5, total, g, k, who=(1,))
    plan(2 * PIECES, -1, add_above, 3)
    starts = [-3 * PIECES + 2 * k for k in high] + [2 * k for k in high]
    starts += [2 * PIECES + 2 * k for k in every]
    jobs = [(2, k) for k in every] + [(3, k) for k in every]
    for start, (g, k) in zip(starts, jobs):
        if (g, k) not in [(2, k) for k in high]:
            plan(start, 0, pass_on, g, k, who=(0,))
            plan(start + 1 + HOP, 1, give, g, k, who=(1,))
        plan(start + 2 + HOP, 2, keep, g, k, who=(1,))
        plan(start + 2 + 2 * HOP, 3, renew, g, k, who=(1,))
        plan(start + 3 + 3 * HOP, 4, spread_other, g, k, who=(1,))
        plan(1000, 5, spread_both, g, k, who=(0,))
    by_role(*both)
    for s in range(2):

        @pl.when(up)
        def _():
            upward[s].wait_send()

        @pl.when(left)
        def _():
            sideways[s].wait_send()

        @pl.when(down & left)
        def _():
            corners[s].wait_send()

    for g in range(4):

        @pl.when(right)
        def _():
            to_right[g].wait_send()

        @pl.when(down)
        def _():
            to_below[g].wait_send()

        for k in every:
            sum_copy(g, k, other_half).wait_send()

            @pl.when(jnp.logical_not(owner))
            def _():
                sum_copy(g, k, own_half).wait_send()

    for g in (2, 3):
        for k in every:

            @pl.when(owner)
            def _():
                new_copy(g, k, own_half, 0).wait_send()

            @pl.when(outer)
            def _():
                new_copy(g, k, own_half, 1).wait_send()
                new_copy(g, k, other_half, 1).wait_send()


def on_device(n_scan, n_tx, n_ty, object_slices, probe_modes, corners, measured):
    layers, side = object_slices.shape[0], object_slices.shape[2]
    modes, pixels = probe_modes.shape[1], probe_modes.shape[-1]
    rim = pixels // 2
    wide = side + rim
    tables = jnp.asarray(dft_tables(pixels))
    tile = object_slices.reshape(2 * layers, side, side)
    anywhere = pl.BlockSpec(memory_space=pl.ANY)
    vmem, dma, f32 = pltpu.VMEM, pltpu.SemaphoreType.DMA, jnp.float32
    pieces = 2 * PIECES
    updated = pl.pallas_call(
        functools.partial(iteration_kernel, n_scan, n_tx, n_ty),
        out_shape=pltpu.VMEM(tile.shape, f32),
        in_specs=[pl.BlockSpec(memory_space=pltpu.SMEM)] + [anywhere] * 4,
        out_specs=pl.BlockSpec(memory_space=pltpu.VMEM),
        scratch_shapes=[
            vmem((2, modes, pixels, pixels), f32),
            vmem((pixels, pixels), f32),
            vmem(tables.shape, tables.dtype),
            vmem((2, wide, wide), f32),
            vmem((2, wide, wide), f32),
            vmem((4, pixels, pixels), f32),
            vmem((2, modes, pixels, pixels), f32),
            vmem((2, modes, pixels, pixels), f32),
            vmem((pixels, pixels), f32),
            vmem((3, 2, wide, pixels), f32),
            vmem((3, 2, wide, side), f32),
            vmem((3, 2, wide, rim), f32),
            vmem((3, 2, wide, rim), f32),
            vmem((3, 2, rim, side), f32),
            vmem((3, 2, side, side), f32),
            vmem((3, 2, side, side), f32),
            dma((5,)), dma((2, 3)), dma((2, 3)), dma((4,)), dma((4,)), dma((4,)), dma((4,)),
            dma((4, pieces, 2)), dma((4, pieces, 2)), dma((4, pieces)),
            dma((2, pieces, 2, 2)), dma((2, pieces, 2)),
        ],
        compiler_params=pltpu.CompilerParams(
            collective_id=0, has_side_effects=True, vmem_limit_bytes=60 * 1024 * 1024),
        name="iteration",
    )(corners[0, 0, 0], tile, probe_modes, measured[0, 0, 0], tables)
    return updated.reshape(object_slices.shape)


def solution(mesh):
    placed = (
        P(None, None, "tx", "ty"),
        P(),
        P("tx", "ty", "scan", None),
        P("tx", "ty", "scan", None, None),
    )
    sizes = (mesh.shape["scan"], mesh.shape["tx"], mesh.shape["ty"])
    return jax.shard_map(
        functools.partial(on_device, *sizes),
        mesh=mesh,
        in_specs=placed,
        out_specs=P(None, None, "tx", "ty"),
        check_vma=False,
    )
```
